512 devices in a mesh: slab: 128 (over x, z, y_hi), head: 4 (over y_lo, core).
Axes of the slice: x: 4, y: 4 (y_hi: 2, y_lo: 2; y = y_hi * 2 + y_lo), z: 16, core: 2. Of those that a mesh axis runs over, the one named last changes fastest.
Arguments:
- query_in: bfloat16 [49152, 3072], P(('slab', 'head')), may hold values from -6 to 6
- key_in: bfloat16 [49152, 3072], P(('slab', 'head')), may hold values from -6 to 6
- value_in: bfloat16 [49152, 3072], P(('slab', 'head')), may hold values from -6 to 6
- grad_out: bfloat16 [49152, 3072], P(('slab', 'head')), may hold values from -6 to 6
- neighbours: int32 [768, 16], P('slab'), may hold values from -1 to 767, as said below
Outputs:
- attended: bfloat16 [49152, 3072], P(('slab', 'head'))
- grad_query: bfloat16 [49152, 3072], P(('slab', 'head'))
- grad_key: bfloat16 [49152, 3072], P(('slab', 'head'))
- grad_value: bfloat16 [49152, 3072], P(('slab', 'head'))
The draws below stay inside these ranges and needn't reach their ends.
Inputs may be any that keep to these rules, and one draw needn't show every extreme that they name: `neighbours`: slab s is tiles s * 6 to (s + 1) * 6 - 1. Row t names distinct key tiles, all in the slab of tile t or in the slabs directly before and after it; its first entry is t itself; -1 marks an unused slot, which names no tile.
All inputs are finite; a program needn't handle non-finite values.
Results may differ from the reference program's by a relative error of at most 0.018.
Values may be sent and summed in bfloat16 or wider, within the bound.
A program may use at most 64 MiB of HBM per device.

```python
import math
import jax
import jax.numpy as jnp
from jax import lax

HEADS = 24
HD = 128
TILE = 64
STILES = 6
NBR = 16
TOKENS = 49152
N_SLAB = 128


def draw_neighbours(key, part):
    tile_total = STILES * N_SLAB
    tile_ids = jnp.arange(tile_total, dtype=jnp.int32)
    slab_of = tile_ids // STILES
    local_pos = tile_ids % STILES
    candidate = jnp.arange(3 * STILES, dtype=jnp.int32)
    key_ids = (slab_of[:, None] - 1) * STILES + candidate[None, :]
    usable = (key_ids >= 0) & (key_ids < tile_total)
    jitter = jax.random.randint(key, (tile_total, 3 * STILES), 0, 1 << 16, dtype=jnp.int32)
    ranking = jitter * 4096 + candidate[None, :]
    same_place = candidate[None, :] % STILES == local_pos[:, None]
    ranking = jnp.where(same_place, (2 << 28) + candidate[None, :], ranking)
    itself = candidate[None, :] == STILES + local_pos[:, None]
    ranking = jnp.where(itself, 3 << 28, ranking)
    ranking = jnp.where(usable, ranking, -1 - candidate[None, :])
    chosen_order = jnp.argsort(-ranking, axis=1, stable=True)[:, :NBR]
    picked = jnp.take_along_axis(key_ids, chosen_order, axis=1)
    picked_ok = jnp.take_along_axis(usable, chosen_order, axis=1)
    return jnp.where(picked_ok, picked, -1).astype(jnp.int32)


def draw_query_in(key, part):
    shape_all = (TOKENS, HEADS * HD)
    values_drawn = jnp.clip(jax.random.normal(jax.random.fold_in(key, 1), shape_all, jnp.float32), -6.0, 6.0)
    return values_drawn.astype(jnp.bfloat16)


def draw_key_in(key, part):
    shape_all = (TOKENS, HEADS * HD)
    values_drawn = jnp.clip(jax.random.normal(jax.random.fold_in(key, 2), shape_all, jnp.float32), -6.0, 6.0)
    return values_drawn.astype(jnp.bfloat16)


def steps_of(rng, shape, cuts, least, largest):
    def one(dim, parts):
        heights = jax.random.uniform(jax.random.fold_in(jax.random.fold_in(rng, 6), dim), (parts,), jnp.float32, least / len(cuts), largest / len(cuts))
        return jnp.repeat(jnp.exp(heights), shape[dim] // parts).reshape((-1,) + (1,) * (len(shape) - dim - 1))

    gain = one(*cuts[0])
    for cut in cuts[1:]:
        gain = gain * one(*cut)
    return gain


def noise(key, dims, deviation, bound, split=(), kind=jnp.bfloat16):
    array = jax.random.normal(key, dims, jnp.float32) * deviation
    if len(split) > 0:
        array = steps_of(key, dims, split, -0.22, 0.18) * array
    return jnp.clip(array, min=-bound, max=bound).astype(kind)


def setup_inputs(seed: int = 0) -> dict:
    arg_keys = jax.random.split(jax.random.key(seed), 6)
    query_in = draw_query_in(jax.random.fold_in(arg_keys[5], 71), 0)
    key_in = draw_key_in(jax.random.fold_in(arg_keys[5], 71), 0)
    value_in = noise(arg_keys[2], (TOKENS, HEADS * HD), 1.0, 6.0, ((0, 512),))
    grad_out = noise(arg_keys[3], (TOKENS, HEADS * HD), 1.0, 6.0, ((0, 512),))
    neighbours = draw_neighbours(jax.random.fold_in(arg_keys[5], 71), 0)
    return {"query_in": query_in, "key_in": key_in, "value_in": value_in, "grad_out": grad_out, "neighbours": neighbours}


def window_mask(id_rows, first_tile, key_count):
    tiles_key = key_count // TILE
    tile_ids = first_tile + jnp.arange(tiles_key, dtype=jnp.int32)
    listed = jnp.any((id_rows[:, :, None] == tile_ids[None, None, :]) & (id_rows[:, :, None] >= 0), axis=1)
    tile_count = id_rows.shape[0]
    spread = jnp.broadcast_to(listed[:, None, :, None], (tile_count, TILE, tiles_key, TILE))
    return spread.reshape(tile_count * TILE, key_count)

def reference(query_in, key_in, value_in, grad_out, neighbours):
    score_scale = 1.0 / math.sqrt(HD)
    full_width = query_in.shape[1]
    head_count = full_width // HD
    slab_rows = STILES * TILE
    zeros_rim = jnp.zeros((slab_rows, full_width), jnp.bfloat16)
    key_pad = jnp.concatenate([zeros_rim, key_in, zeros_rim], axis=0)
    val_pad = jnp.concatenate([zeros_rim, value_in, zeros_rim], axis=0)
    acc_zero = jnp.zeros((key_in.shape[0] + 2 * slab_rows, 2 * full_width), jnp.float32)

    def slab_step(grad_acc, slab_index):
        row_start = (slab_index * slab_rows).astype(jnp.int32)
        query_rows = lax.dynamic_slice_in_dim(query_in, row_start, slab_rows, 0)
        grad_rows = lax.dynamic_slice_in_dim(grad_out, row_start, slab_rows, 0)
        id_rows = lax.dynamic_slice_in_dim(neighbours, (slab_index * STILES).astype(jnp.int32), STILES, 0)
        key_win = lax.dynamic_slice_in_dim(key_pad, row_start, 3 * slab_rows, 0)
        val_win = lax.dynamic_slice_in_dim(val_pad, row_start, 3 * slab_rows, 0)
        first_tile = ((slab_index - 1) * STILES).astype(jnp.int32)
        allowed = window_mask(id_rows, first_tile, 3 * slab_rows)[None]
        query_heads = query_rows.reshape(slab_rows, head_count, HD).astype(jnp.float32)
        grad_heads = grad_rows.reshape(slab_rows, head_count, HD).astype(jnp.float32)
        key_heads = key_win.reshape(3 * slab_rows, head_count, HD).astype(jnp.float32)
        val_heads = val_win.reshape(3 * slab_rows, head_count, HD).astype(jnp.float32)
        scores = jnp.einsum('qhd,khd->hqk', query_heads, key_heads) * score_scale
        scores = jnp.where(allowed, scores, -1e+30)
        row_peak = lax.optimization_barrier(jnp.max(scores, axis=2, keepdims=True))
        log_total = row_peak + jnp.log(lax.optimization_barrier(jnp.sum(jnp.exp(scores - row_peak), axis=2, keepdims=True)))
        weights = jnp.where(allowed, jnp.exp(scores - log_total), 0.0)
        weights_low = weights.astype(jnp.bfloat16).astype(jnp.float32)
        out_heads = jnp.einsum('hqk,khd->qhd', weights_low, val_heads).astype(jnp.bfloat16)
        out_dot = lax.optimization_barrier(jnp.sum(grad_heads * out_heads.astype(jnp.float32), axis=2))
        dweights = jnp.einsum('qhd,khd->hqk', grad_heads, val_heads)
        dscores = (weights * (dweights - out_dot.T[:, :, None])).astype(jnp.bfloat16).astype(jnp.float32)
        dq_heads = (jnp.einsum('hqk,khd->qhd', dscores, key_heads) * score_scale).astype(jnp.bfloat16)
        dk_win = jnp.einsum('hqk,qhd->khd', dscores, query_heads) * score_scale
        dv_win = jnp.einsum('hqk,qhd->khd', weights_low, grad_heads)
        stacked = jnp.concatenate([dk_win.reshape(3 * slab_rows, full_width), dv_win.reshape(3 * slab_rows, full_width)], axis=1)
        current = lax.dynamic_slice_in_dim(grad_acc, row_start, 3 * slab_rows, 0)
        grad_acc = lax.dynamic_update_slice_in_dim(grad_acc, current + stacked, row_start, 0)
        return (grad_acc, (out_heads.reshape(slab_rows, full_width), dq_heads.reshape(slab_rows, full_width)))
    grad_acc, (out_rows, dq_rows) = lax.scan(slab_step, acc_zero, jnp.arange(N_SLAB, dtype=jnp.int32))
    inner = grad_acc[slab_rows:slab_rows + key_in.shape[0]]
    attended = out_rows.reshape(key_in.shape[0], full_width)
    grad_query = dq_rows.reshape(key_in.shape[0], full_width)
    grad_key = inner[:, :full_width].astype(jnp.bfloat16)
    grad_value = inner[:, full_width:].astype(jnp.bfloat16)
    return (attended, grad_query, grad_key, grad_value)
```

```python
import functools
import math

import jax
import jax.numpy as jnp
from jax import lax
from jax.experimental import pallas as pl
from jax.experimental.pallas import tpu as pltpu
from jax.sharding import PartitionSpec as P

HD = 128
TILE = 64
MESH = pl.DeviceIdType.MESH
F32 = jnp.float32
BF16 = jnp.bfloat16
NEG = -1e30

NN = (((1,), (0,)), ((), ()))
NT = (((1,), (1,)), ((), ()))
TN = (((0,), (0,)), ((), ()))


def dot(a, b, dims):
    return lax.dot_general(a, b, dims, preferred_element_type=F32)


def attend_head(i, kv, qd, bias, s_scr, p_scr, d_scr, own32, near32, far16, outs):
    rows = qd.shape[2]
    tiles = rows // TILE
    scale = 1.0 / math.sqrt(HD)
    c = scale * math.log2(math.e)
    query = qd[i, 0]
    peak = None
    for b in range(3):
        s = dot(kv[b, i, 0], query, NT)
        s = s.reshape(tiles, TILE // 8, 8, rows) + bias[b * tiles : (b + 1) * tiles][:, None]
        top = jnp.max(s, axis=(0, 1))
        peak = top if peak is None else jnp.maximum(peak, top)
        s_scr[b * rows : (b + 1) * rows] = s.reshape(rows, rows)
    peak = jnp.max(peak, axis=0, keepdims=True)
    total = None
    out_t = None
    for b in range(3):
        part = slice(b * rows, (b + 1) * rows)
        e = jnp.exp2((s_scr[part] - peak) * c)
        t = jnp.sum(e.reshape(rows // 8, 8, rows), axis=0)
        total = t if total is None else total + t
        low = e.astype(BF16)
        p_scr[part] = low
        s_scr[part] = e
        o = dot(kv[b, i, 1], low, TN)
        out_t = o if out_t is None else out_t + o
    inv = 1.0 / jnp.sum(total, axis=0, keepdims=True)
    out_low = (out_t * inv).astype(BF16).astype(F32)
    outs[0, i] = out_low.T.astype(BF16)
    grad_t = qd[i, 1].astype(F32).T * inv
    grad_n = grad_t.T.astype(BF16)
    delta = jnp.sum(grad_t * out_low, axis=0, keepdims=True)
    dq_t = None
    for b in range(3):
        part = slice(b * rows, (b + 1) * rows)
        dp = dot(kv[b, i, 1], grad_n, NT)
        ds = (s_scr[part] * (dp - delta)).astype(BF16)
        dk = dot(ds, query, NN) * scale
        dv = dot(p_scr[part], grad_n, NN)
        if b == 2:
            far16[i, 0] = dk.astype(BF16)
            far16[i, 1] = dv.astype(BF16)
        else:
            held = own32 if b == 0 else near32
            held[i, 0] = dk
            held[i, 1] = dv
        g = dot(kv[b, i, 0], ds, TN)
        dq_t = g if dq_t is None else dq_t + g
    outs[1, i] = (dq_t * scale).T.astype(BF16)


def kernel(n, nbr, q, k, v, do, o_att, o_dq, o_dk, o_dv,
           kv, qd, bias, s_scr, p_scr, d_scr, own32, near32, far16, near16, gfar, gnear, outs,
           kv_in, qd_in, kv_out, qd_out, sa, ra, sb, rb, sc, rc, sd, rd, so, ro, lo):
    block = q.shape[0]
    rows = qd.shape[2]
    heads = qd.shape[0]
    tiles = rows // TILE
    width = heads * HD
    s = lax.axis_index("slab")
    h = lax.axis_index("head")
    odd = lax.rem(s, 2)
    near = s + 1 - 2 * odd
    onward = lax.rem(s + 2 - 4 * odd + n, n)
    source = lax.rem(s - 2 + 4 * odd + n, n)
    across = lax.rem(h + 2, 4)
    beside = h + 1 - 2 * lax.rem(h, 2)
    slab_peers = (s, lax.rem(beside + 2, 4)), (s, across), (s, beside)
    near_id, onward_id, source_id = (near, across), (onward, h), (source, h)

    def group(head):
        return lax.rem(head + 2 * odd, 4)

    def columns(head, i):
        return pl.ds(pl.multiple_of(group(head) * width + i * HD, HD), HD)

    def block_of(head):
        return pl.ds(pl.multiple_of(head * block, 32), block)

    barrier = pltpu.get_barrier_semaphore()
    for peer in slab_peers + (near_id, onward_id, source_id):
        pl.semaphore_signal(barrier, inc=1, device_id=peer, device_id_type=MESH)

    lane_tile = lax.broadcasted_iota(jnp.int32, (8, rows), 1) // TILE
    far_first = jnp.where(s == 0, -1000, (s - 1 + 2 * odd) * tiles)
    firsts = (s * tiles, near * tiles, far_first)
    listed = []
    for slot in range(nbr.shape[1]):
        row = jnp.full((8, rows), nbr[0, slot], jnp.int32)
        for t in range(1, tiles):
            row = jnp.where(lane_tile == t, nbr[t, slot], row)
        listed.append(row)
    for b in range(3):
        for t in range(tiles):
            hit = listed[0] == firsts[b] + t
            for row in listed[1:]:
                hit = hit | (row == firsts[b] + t)
            bias[b * tiles + t] = jnp.where(hit, 0.0, NEG)

    pl.semaphore_wait(barrier, 6)

    def send(src, dst, s_sem, r_sem, peer):
        pltpu.make_async_remote_copy(
            src_ref=src, dst_ref=dst, send_sem=s_sem, recv_sem=r_sem,
            device_id=peer, device_id_type=MESH,
        ).start()

    def arrive(ref, sem):
        pltpu.make_async_copy(ref, ref, sem).wait()

    def spread(i, pair, into, s_sem, r_sem):
        for peer in slab_peers:
            for a, ref in enumerate(pair):
                send(ref.at[:, columns(peer[1], i)], into.at[i, a, block_of(h), :],
                     s_sem.at[i], r_sem.at[i], peer)
        for a, ref in enumerate(pair):
            pltpu.make_async_copy(
                ref.at[:, columns(h, i)], into.at[i, a, block_of(h), :], r_sem.at[i]
            ).start()

    own = kv.at[0]

    @pl.loop(0, heads)
    def _(i):
        spread(i, (k, v), own, kv_out, kv_in)

    @pl.loop(0, heads)
    def _(i):
        spread(i, (q, do), qd, qd_out, qd_in)

    def gather(i, a, out, r):
        for peer in slab_peers:
            send(outs.at[a, i, block_of(peer[1]), :], out.at[:, columns(h, i)],
                 so.at[a], ro.at[a], peer)
        pltpu.make_async_copy(
            outs.at[a, i, block_of(h), :], out.at[:, columns(h, i)], lo.at[a]
        ).start()

    def ship(i):
        arrive(kv.at[0, i], kv_in.at[i])
        send(kv.at[0, i], kv.at[1, i], sa.at[i], ra.at[i], near_id)

    def relay(i):
        arrive(kv.at[1, i], ra.at[i])
        send(kv.at[1, i], kv.at[2, i], sb.at[i], rb.at[i], onward_id)

    def compute(i):
        arrive(kv.at[2, i], rb.at[i])
        arrive(qd.at[i], qd_in.at[i])
        attend_head(i, kv, qd, bias, s_scr, p_scr, d_scr, own32, near32, far16, outs)
        send(far16.at[i], gfar.at[i], sc.at[i], rc.at[i], source_id)
        gather(i, 0, o_att, 0)
        gather(i, 1, o_dq, 1)

    def fold(i):
        arrive(gfar.at[i], rc.at[i])
        near16[i] = (near32[i] + gfar[i].astype(F32)).astype(BF16)
        send(near16.at[i], gnear.at[i], sd.at[i], rd.at[i], near_id)

    def finish(i):
        arrive(gnear.at[i], rd.at[i])
        done = (own32[i] + gnear[i].astype(F32)).astype(BF16)
        outs[2, i] = done[0]
        outs[3, i] = done[1]
        gather(i, 2, o_dk, 2)
        gather(i, 3, o_dv, 3)

    ship(0)
    ship(1)

    @pl.loop(0, heads + 5)
    def _(step):
        for lag, task in ((-2, ship), (0, relay), (5, finish), (3, fold), (1, compute)):
            i = step - lag

            @pl.when((i >= (2 if lag < 0 else 0)) & (i < heads))
            def _():
                task(i)

    for i in range(heads):
        arrive(kv.at[0, i, :, 0 : 3 * block], kv_out.at[i])
        arrive(qd.at[i, :, 0 : 3 * block], qd_out.at[i])
        arrive(kv.at[0, i], sa.at[i])
        arrive(kv.at[1, i], sb.at[i])
        arrive(far16.at[i], sc.at[i])
        arrive(near16.at[i], sd.at[i])
    for a in range(4):
        arrive(outs.at[a, :, 0 : 3 * block], so.at[a])
        arrive(outs.at[a, :, 0 : 3 * block], ro.at[a])
        arrive(outs.at[a, :, 0:block], lo.at[a])


def solution(mesh):
    n = mesh.shape["slab"]
    parts = mesh.shape["head"]

    def step(query_in, key_in, value_in, grad_out, neighbours):
        block, full = query_in.shape
        rows = block * parts
        heads = full // parts // HD
        tiles = rows // TILE
        shape = jax.ShapeDtypeStruct((block, full), BF16)
        pair16 = pltpu.VMEM((heads, 2, rows, HD), BF16)
        pair32 = pltpu.VMEM((heads, 2, rows, HD), F32)
        each = pltpu.SemaphoreType.DMA((heads,))
        four = pltpu.SemaphoreType.DMA((4,))
        return pl.pallas_call(
            functools.partial(kernel, n),
            out_shape=(shape,) * 4,
            in_specs=[pl.BlockSpec(memory_space=pltpu.SMEM)]
            + [pl.BlockSpec(memory_space=pl.ANY)] * 4,
            out_specs=(pl.BlockSpec(memory_space=pl.ANY),) * 4,
            scratch_shapes=[
                pltpu.VMEM((3, heads, 2, rows, HD), BF16),
                pair16,
                pltpu.VMEM((3 * tiles, 8, rows), F32),
                pltpu.VMEM((3 * rows, rows), F32),
                pltpu.VMEM((3 * rows, rows), BF16),
                pltpu.VMEM((8, HD), BF16),
                pair32, pair32,
                pair16, pair16, pair16, pair16,
                pltpu.VMEM((4, heads, rows, HD), BF16),
            ] + [each] * 12 + [four] * 3,
            compiler_params=pltpu.CompilerParams(
                collective_id=0, has_side_effects=True, vmem_limit_bytes=60 * 1024 * 1024
            ),
        )(neighbours, query_in, key_in, value_in, grad_out)

    rows_spec = P(("slab", "head"), None)
    return jax.shard_map(
        step, mesh=mesh, in_specs=(rows_spec,) * 4 + (P("slab", None),),
        out_specs=(rows_spec,) * 4, check_vma=False,
    )
```

```python
import functools
import math

import jax
import jax.numpy as jnp
from jax import lax
from jax.experimental import pallas as pl
from jax.experimental.pallas import tpu as pltpu
from jax.sharding import PartitionSpec as P

HD = 128
TILE = 64
MESH = pl.DeviceIdType.MESH
F32 = jnp.float32
BF16 = jnp.bfloat16
NEG = -1e30

NN = (((1,), (0,)), ((), ()))
NT = (((1,), (1,)), ((), ()))
TN = (((0,), (0,)), ((), ()))


def dot(a, b, dims):
    return lax.dot_general(a, b, dims, preferred_element_type=F32)


def attend_head(i, kv, qd, bias, s_scr, p_scr, own32, near32, far16, outs):
    rows = qd.shape[2]
    tiles = rows // TILE
    scale = 1.0 / math.sqrt(HD)
    c = scale * math.log2(math.e)
    query = qd[i, 0]
    peak = None
    for b in range(3):
        s = dot(kv[b, i, 0], query, NT)
        s = s.reshape(tiles, TILE // 8, 8, rows) + bias[b * tiles : (b + 1) * tiles][:, None]
        top = jnp.max(s, axis=(0, 1))
        peak = top if peak is None else jnp.maximum(peak, top)
        s_scr[b * rows : (b + 1) * rows] = s.reshape(rows, rows)
    peak = jnp.max(peak, axis=0, keepdims=True)
    total = None
    out_t = None
    for b in range(3):
        part = slice(b * rows, (b + 1) * rows)
        e = jnp.exp2((s_scr[part] - peak) * c)
        t = jnp.sum(e.reshape(rows // 8, 8, rows), axis=0)
        total = t if total is None else total + t
        low = e.astype(BF16)
        p_scr[part] = low
        s_scr[part] = e
        o = dot(kv[b, i, 1], low, TN)
        out_t = o if out_t is None else out_t + o
    inv = 1.0 / jnp.sum(total, axis=0, keepdims=True)
    out_low = (out_t * inv).astype(BF16).astype(F32)
    outs[0, i] = out_low.T.astype(BF16)
    grad_t = qd[i, 1].astype(F32).T * inv
    grad_n = grad_t.T.astype(BF16)
    delta = jnp.sum(grad_t * out_low, axis=0, keepdims=True)
    dq_t = None
    for b in range(3):
        part = slice(b * rows, (b + 1) * rows)
        dp = dot(kv[b, i, 1], grad_n, NT)
        ds = (s_scr[part] * (dp - delta)).astype(BF16)
        dk = dot(ds, query, NN) * scale
        dv = dot(p_scr[part], grad_n, NN)
        if b == 2:
            far16[i, 0] = dk.astype(BF16)
            far16[i, 1] = dv.astype(BF16)
        else:
            held = own32 if b == 0 else near32
            held[i, 0] = dk
            held[i, 1] = dv
        g = dot(kv[b, i, 0], ds, TN)
        dq_t = g if dq_t is None else dq_t + g
    outs[1, i] = (dq_t * scale).T.astype(BF16)


def kernel(n, listing, q, k, v, do, o_att, o_dq, o_dk, o_dv,
           kv, qd, bias, s_scr, p_scr, own32, near32, far16, near16, gfar, gnear, outs,
           kv_own, kv_beside, kv_cross, kv_out, qd_in, qd_out,
           sa, ra, sb, rb, sc, rc, sd, rd, so, ro, lo, ready, nbr, nbr_in):
    block = q.shape[0]
    rows = qd.shape[2]
    heads = qd.shape[0]
    tiles = rows // TILE
    width = heads * HD
    s = lax.axis_index("slab")
    h = lax.axis_index("head")
    odd = lax.rem(s, 2)
    near = s + 1 - 2 * odd
    above = lax.rem(s + 2, n)
    below = lax.rem(s - 2 + n, n)
    onward = jnp.where(odd == 0, above, below)
    source = jnp.where(odd == 0, below, above)
    across = lax.rem(h + 2, 4)
    beside = h + 1 - 2 * lax.rem(h, 2)
    slab_peers = (s, across), (s, lax.rem(beside + 2, 4)), (s, beside)
    near_id, onward_id, source_id = (near, across), (onward, h), (source, h)
    depth = min(16, n // 2)
    level = lax.rem(s // 2, depth)
    first = jnp.where(level == 0, 1, 0)
    last = jnp.where(level == depth - 1, 1, 0)

    def group(head):
        return lax.rem(head + 2 * odd, 4)

    def columns(head, i):
        return pl.ds(pl.multiple_of(group(head) * width + i * HD, HD), HD)

    def block_of(head):
        return pl.ds(pl.multiple_of(head * block, 32), block)

    cross_rows = pl.ds(pl.multiple_of((1 - h // 2) * (2 * block), 32), 2 * block)

    def signal(sem, peer):
        pl.semaphore_signal(sem, inc=1, device_id=peer, device_id_type=MESH)

    barrier = pltpu.get_barrier_semaphore()
    for peer in slab_peers + (near_id,):
        signal(barrier, peer)

    @pl.when(last == 0)
    def _():
        signal(barrier, (above, h))

    @pl.when(first == 1)
    def _():
        signal(barrier, (below, h))

    pl.semaphore_wait(barrier, 5 - first + last)

    def send(src, dst, s_sem, r_sem, peer):
        pltpu.make_async_remote_copy(
            src_ref=src, dst_ref=dst, send_sem=s_sem, recv_sem=r_sem,
            device_id=peer, device_id_type=MESH,
        ).start()

    def arrive(ref, sem):
        pltpu.make_async_copy(ref, ref, sem).wait()

    def spread(i, pair, into, out, sems, mine):
        for peer, sem in zip(slab_peers, sems):
            for a, ref in enumerate(pair):
                send(ref.at[:, columns(peer[1], i)], into.at[i, a, block_of(h), :],
                     out.at[i], sem.at[i], peer)
        for a, ref in enumerate(pair):
            pltpu.make_async_copy(
                ref.at[:, columns(h, i)], into.at[i, a, block_of(h), :], mine.at[i]
            ).start()

    def spread_kv(i):
        spread(i, (k, v), kv.at[0], kv_out, (kv_cross, kv_cross, kv_beside), kv_own)

    def spread_qd(i):
        spread(i, (q, do), qd, qd_out, (qd_in, qd_in, qd_in), qd_in)

    def ship_held(i):
        for a, ref in enumerate((k, v)):
            send(ref.at[:, columns(h, i)], kv.at[1, i, a, block_of(h), :], sa.at[i], ra.at[i], near_id)

    def ship_beside(i):
        part = kv.at[0, i, :, block_of(beside), :]
        arrive(part, kv_beside.at[i])
        send(part, kv.at[1, i, :, block_of(beside), :], sa.at[i], ra.at[i], near_id)

    def ship_cross(i):
        part = kv.at[0, i, :, cross_rows, :]
        arrive(part, kv_cross.at[i])
        send(part, kv.at[1, i, :, cross_rows, :], sa.at[i], ra.at[i], near_id)

    def gather(i, a, out):
        for peer in slab_peers:
            send(outs.at[a, i, block_of(peer[1]), :], out.at[:, columns(h, i)],
                 so.at[a], ro.at[a], peer)
        pltpu.make_async_copy(
            outs.at[a, i, block_of(h), :], out.at[:, columns(h, i)], lo.at[a]
        ).start()

    def relay(i):
        arrive(kv.at[1, i], ra.at[i])
        send(kv.at[1, i], kv.at[2, i], sb.at[i], rb.at[i], onward_id)

    def compute(i):
        arrive(kv.at[0, i, :, block_of(h), :], kv_own.at[i])
        arrive(qd.at[i], qd_in.at[i])
        arrive(kv.at[2, i], rb.at[i])
        attend_head(i, kv, qd, bias, s_scr, p_scr, own32, near32, far16, outs)

        @pl.when((i == 0) & (jnp.where(odd == 0, first, 1 - last) == 1))
        def _():
            pl.semaphore_wait(ready.at[1], 1)

        send(far16.at[i], gfar.at[i], sc.at[i], rc.at[i], source_id)
        gather(i, 0, o_att)
        gather(i, 1, o_dq)

    def fold(i):
        arrive(gfar.at[i], rc.at[i])
        for a in range(2):
            near16[i, a] = (near32[i, a] + gfar[i, a].astype(F32)).astype(BF16)
            send(near16.at[i, a], gnear.at[i, a], sd.at[i], rd.at[i, a], near_id)

    def finish(i):
        for a, out in enumerate((o_dk, o_dv)):
            arrive(gnear.at[i, a], rd.at[i, a])
            outs[2 + a, i] = (own32[i, a] + gnear[i, a].astype(F32)).astype(BF16)
            gather(i, 2 + a, out)

    def ship_on(i):
        ship_cross(i)

        @pl.when(i + 1 < heads)
        def _():
            ship_held(i + 1)
            ship_beside(i + 1)

    listing_copy = pltpu.make_async_copy(listing, nbr, nbr_in)
    listing_copy.start()

    spread_kv(0)
    ship_held(0)
    spread_kv(1)
    ship_held(1)
    spread_kv(2)
    for i in range(3, heads):
        spread_qd(i - 3)
        spread_kv(i)
    for i in range(max(heads - 3, 0), heads):
        spread_qd(i)

    @pl.when(first == 0)
    def _():
        signal(ready.at[odd], (below, h))

    @pl.when(last == 1)
    def _():
        signal(ready.at[1 - odd], (above, h))

    ship_beside(0)
    ship_beside(1)

    listing_copy.wait()
    lane_tile = lax.broadcasted_iota(jnp.int32, (8, rows), 1) // TILE
    far_first = jnp.where(s == 0, -1000, (s - 1 + 2 * odd) * tiles)
    firsts = (s * tiles, near * tiles, far_first)
    listed = []
    for slot in range(nbr.shape[1]):
        row = jnp.full((8, rows), nbr[0, slot], jnp.int32)
        for t in range(1, tiles):
            row = jnp.where(lane_tile == t, nbr[t, slot], row)
        listed.append(row)
    for b in range(3):
        for t in range(tiles):
            hit = listed[0] == firsts[b] + t
            for row in listed[1:]:
                hit = hit | (row == firsts[b] + t)
            bias[b * tiles + t] = jnp.where(hit, 0.0, NEG)

    ship_cross(0)
    ship_on(1)

    @pl.when(jnp.where(odd == 0, 1 - last, first) == 1)
    def _():
        pl.semaphore_wait(ready.at[0], 1)

    relay(0)
    ship_on(2)

    hold = 2 * first * (1 - odd)
    turn = first * odd

    @pl.loop(0, heads + 6)
    def _(step):
        for start, lag, task in ((1, -1, relay), (3, -3, ship_on), (0, 3 + turn, fold), (0, hold, compute), (0, 6, finish)):
            i = step - lag

            @pl.when((i >= start) & (i < heads))
            def _():
                task(i)

    for i in range(heads):
        arrive(kv.at[0, i, :, 0 : 3 * block], kv_out.at[i])
        arrive(qd.at[i, :, 0 : 3 * block], qd_out.at[i])
        arrive(kv.at[0, i], sa.at[i])
        arrive(kv.at[1, i], sb.at[i])
        arrive(far16.at[i], sc.at[i])
        arrive(near16.at[i], sd.at[i])
    for a in range(4):
        arrive(outs.at[a, :, 0 : 3 * block], so.at[a])
        arrive(outs.at[a, :, 0 : 3 * block], ro.at[a])
        arrive(outs.at[a, :, 0:block], lo.at[a])


def solution(mesh):
    n = mesh.shape["slab"]
    parts = mesh.shape["head"]

    def step(query_in, key_in, value_in, grad_out, neighbours):
        block, full = query_in.shape
        rows = block * parts
        heads = full // parts // HD
        tiles = rows // TILE
        shape = jax.ShapeDtypeStruct((block, full), BF16)
        pair16 = pltpu.VMEM((heads, 2, rows, HD), BF16)
        pair32 = pltpu.VMEM((heads, 2, rows, HD), F32)
        each = pltpu.SemaphoreType.DMA((heads,))
        four = pltpu.SemaphoreType.DMA((4,))
        held = pl.pallas_call(
            functools.partial(kernel, n),
            out_shape=(pltpu.VMEM((block, full), BF16),) * 4,
            in_specs=[pl.BlockSpec(memory_space=pl.ANY)] * 5,
            out_specs=(pl.BlockSpec(memory_space=pltpu.VMEM),) * 4,
            scratch_shapes=[
                pltpu.VMEM((3, heads, 2, rows, HD), BF16),
                pair16,
                pltpu.VMEM((3 * tiles, 8, rows), F32),
                pltpu.VMEM((3 * rows, rows), F32),
                pltpu.VMEM((3 * rows, rows), BF16),
                pair32, pair32,
                pair16, pair16, pair16, pair16,
                pltpu.VMEM((4, heads, rows, HD), BF16),
            ] + [each] * 13 + [pltpu.SemaphoreType.DMA((heads, 2))] + [four] * 3
            + [pltpu.SemaphoreType.REGULAR((2,)), pltpu.SMEM(neighbours.shape, jnp.int32),
               pltpu.SemaphoreType.DMA],
            compiler_params=pltpu.CompilerParams(
                collective_id=0, has_side_effects=True, vmem_limit_bytes=61 * 1024 * 1024 + 512 * 1024
            ),
        )(neighbours, query_in, key_in, value_in, grad_out)
        return held

    rows_spec = P(("slab", "head"), None)
    return jax.shard_map(
        step, mesh=mesh, in_specs=(rows_spec,) * 4 + (P("slab", None),),
        out_specs=(rows_spec,) * 4, check_vma=False,
    )
```

```python
import functools
import math

import jax
import jax.numpy as jnp
from jax import lax
from jax.experimental import pallas as pl
from jax.experimental.pallas import tpu as pltpu
from jax.sharding import PartitionSpec as P

HD = 128
TILE = 64
MESH = pl.DeviceIdType.MESH
F32 = jnp.float32
BF16 = jnp.bfloat16
NEG = -1e30

NN = (((1,), (0,)), ((), ()))
NT = (((1,), (1,)), ((), ()))
TN = (((0,), (0,)), ((), ()))


def dot(a, b, dims):
    return lax.dot_general(a, b, dims, preferred_element_type=F32)


def attend_head(i, kv, qd, bias, s_scr, p_scr, own32, near32, far16, outs):
    rows = qd.shape[2]
    tiles = rows // TILE
    scale = 1.0 / math.sqrt(HD)
    c = scale * math.log2(math.e)
    query = qd[i, 0]
    peak = None
    for b in range(3):
        s = dot(kv[b, i, 0], query, NT)
        s = s.reshape(tiles, TILE // 8, 8, rows) + bias[b * tiles : (b + 1) * tiles][:, None]
        top = jnp.max(s, axis=(0, 1))
        peak = top if peak is None else jnp.maximum(peak, top)
        s_scr[b * rows : (b + 1) * rows] = s.reshape(rows, rows)
    peak = jnp.max(peak, axis=0, keepdims=True)
    total = None
    out_t = None
    for b in range(3):
        part = slice(b * rows, (b + 1) * rows)
        e = jnp.exp2((s_scr[part] - peak) * c)
        t = jnp.sum(e.reshape(rows // 8, 8, rows), axis=0)
        total = t if total is None else total + t
        low = e.astype(BF16)
        p_scr[part] = low
        s_scr[part] = e
        o = dot(kv[b, i, 1], low, TN)
        out_t = o if out_t is None else out_t + o
    inv = 1.0 / jnp.sum(total, axis=0, keepdims=True)
    out_low = (out_t * inv).astype(BF16).astype(F32)
    outs[0, i] = out_low.T.astype(BF16)
    grad_t = qd[i, 1].astype(F32).T * inv
    grad_n = grad_t.T.astype(BF16)
    delta = jnp.sum(grad_t * out_low, axis=0, keepdims=True)
    dq_t = None
    for b in range(3):
        part = slice(b * rows, (b + 1) * rows)
        dp = dot(kv[b, i, 1], grad_n, NT)
        ds = (s_scr[part] * (dp - delta)).astype(BF16)
        dk = dot(ds, query, NN) * scale
        dv = dot(p_scr[part], grad_n, NN)
        if b == 2:
            far16[i, 0] = dk.astype(BF16)
            far16[i, 1] = dv.astype(BF16)
        else:
            held = own32 if b == 0 else near32
            held[i, 0] = dk
            held[i, 1] = dv
        g = dot(kv[b, i, 0], ds, TN)
        dq_t = g if dq_t is None else dq_t + g
    outs[1, i] = (dq_t * scale).T.astype(BF16)


def kernel(n, listing, q, k, v, do, o_att, o_dq, o_dk, o_dv,
           kv, qd, bias, s_scr, p_scr, own32, near32, far16, near16, gfar, gnear, outs,
           kv_own, kv_beside, kv_cross, kv_out, qd_in, qd_out,
           sa, ra, sb, rb, sc, rc, sd, rd, so, ro, lo, ready, nbr, nbr_in):
    block = q.shape[0]
    rows = qd.shape[2]
    heads = qd.shape[0]
    tiles = rows // TILE
    width = heads * HD
    s = lax.axis_index("slab")
    h = lax.axis_index("head")
    odd = lax.rem(s, 2)
    near = s + 1 - 2 * odd
    above = lax.rem(s + 2, n)
    below = lax.rem(s - 2 + n, n)
    onward = jnp.where(odd == 0, above, below)
    source = jnp.where(odd == 0, below, above)
    across = lax.rem(h + 2, 4)
    beside = h + 1 - 2 * lax.rem(h, 2)
    slab_peers = (s, across), (s, lax.rem(beside + 2, 4)), (s, beside)
    near_id, onward_id, source_id = (near, across), (onward, h), (source, h)
    depth = min(16, n // 2)
    level = lax.rem(s // 2, depth)
    first = jnp.where(level == 0, 1, 0)
    last = jnp.where(level == depth - 1, 1, 0)
    lone = (s == 0) | (s == n - 1)
    single = (s == 1) | (s == n - 2)

    def group(head):
        return lax.rem(head + 2 * odd, 4)

    def columns(head, i):
        return pl.ds(pl.multiple_of(group(head) * width + i * HD, HD), HD)

    def block_of(head):
        return pl.ds(pl.multiple_of(head * block, 32), block)

    cross_rows = pl.ds(pl.multiple_of((1 - h // 2) * (2 * block), 32), 2 * block)
    local_rows = pl.ds(pl.multiple_of((h // 2) * (2 * block), 32), 2 * block)

    def signal(sem, peer):
        pl.semaphore_signal(sem, inc=1, device_id=peer, device_id_type=MESH)

    barrier = pltpu.get_barrier_semaphore()
    for peer in slab_peers + (near_id,):
        signal(barrier, peer)

    @pl.when(last == 0)
    def _():
        signal(barrier, (above, h))

    @pl.when(first == 1)
    def _():
        signal(barrier, (below, h))

    pl.semaphore_wait(barrier, 5 - first + last)

    def send(src, dst, s_sem, r_sem, peer):
        pltpu.make_async_remote_copy(
            src_ref=src, dst_ref=dst, send_sem=s_sem, recv_sem=r_sem,
            device_id=peer, device_id_type=MESH,
        ).start()

    def arrive(ref, sem):
        pltpu.make_async_copy(ref, ref, sem).wait()

    def spread(i, pair, into, out, sems, mine):
        for peer, sem in zip(slab_peers, sems):
            for a, ref in enumerate(pair):
                send(ref.at[:, columns(peer[1], i)], into.at[i, a, block_of(h), :],
                     out.at[i], sem.at[i], peer)
        for a, ref in enumerate(pair):
            pltpu.make_async_copy(
                ref.at[:, columns(h, i)], into.at[i, a, block_of(h), :], mine.at[i]
            ).start()

    def spread_kv(i):
        spread(i, (k, v), kv.at[0], kv_out, (kv_cross, kv_cross, kv_beside), kv_own)

    def spread_qd(i):
        spread(i, (q, do), qd, qd_out, (qd_in, qd_in, qd_in), qd_in)

    def ship_held(i):
        for a, ref in enumerate((k, v)):
            send(ref.at[:, columns(h, i)], kv.at[1, i, a, block_of(h), :], sa.at[i], ra.at[i], near_id)

    def ship_beside(i):
        part = kv.at[0, i, :, block_of(beside), :]
        arrive(part, kv_beside.at[i])
        send(part, kv.at[1, i, :, block_of(beside), :], sa.at[i], ra.at[i], near_id)

    def ship_cross(i):
        part = kv.at[0, i, :, cross_rows, :]
        arrive(part, kv_cross.at[i])
        send(part, kv.at[1, i, :, cross_rows, :], sa.at[i], ra.at[i], near_id)

    def gather(i, a, out, peers, mine):
        for peer in peers:
            send(outs.at[a, i, block_of(peer[1]), :], out.at[:, columns(h, i)],
                 so.at[a], ro.at[a], peer)
        if mine:
            pltpu.make_async_copy(
                outs.at[a, i, block_of(h), :], out.at[:, columns(h, i)], lo.at[a]
            ).start()

    def relay(i):
        arrive(kv.at[1, i], ra.at[i])

        @pl.when(jnp.logical_not(single))
        def _():
            send(kv.at[1, i], kv.at[2, i], sb.at[i], rb.at[i], onward_id)

        @pl.when(lone)
        def _():
            pltpu.make_async_copy(kv.at[1, i], kv.at[2, i], rb.at[i]).start()

    def compute(i):
        arrive(kv.at[0, i, :, block_of(h), :], kv_own.at[i])
        arrive(qd.at[i], qd_in.at[i])
        arrive(kv.at[2, i], rb.at[i])
        attend_head(i, kv, qd, bias, s_scr, p_scr, own32, near32, far16, outs)

        @pl.when((i == 0) & (jnp.where(odd == 0, first, 1 - last) == 1) & (s > 0))
        def _():
            pl.semaphore_wait(ready.at[1], 1)

        @pl.when(jnp.logical_not(lone))
        def _():
            for a in range(2):
                send(far16.at[i, a], gfar.at[i, a], sc.at[i], rc.at[i, a], source_id)

        gather(i, 0, o_att, slab_peers, True)
        gather(i, 1, o_dq, slab_peers, True)

    def fold(i):
        for a in range(2):
            @pl.when(jnp.logical_not(single))
            def _():
                arrive(gfar.at[i, a], rc.at[i, a])
                near16[i, a] = (near32[i, a] + gfar[i, a].astype(F32)).astype(BF16)

            @pl.when(single)
            def _():
                near16[i, a] = near32[i, a].astype(BF16)

            if a == 0:
                send(near16.at[i, a], gnear.at[i, a], sd.at[i], rd.at[i, a], near_id)
            else:
                for piece, part in ((1, local_rows), (2, cross_rows)):
                    send(near16.at[i, a, part, :], gnear.at[i, a, part, :], sd.at[i], rd.at[i, piece], near_id)

    def settle(i, a, part):
        outs[2 + a, i, part, :] = (own32[i, a, part, :] + gnear[i, a, part, :].astype(F32)).astype(BF16)

    def finish(i):
        arrive(gnear.at[i, 0], rd.at[i, 0])
        settle(i, 0, slice(None))
        gather(i, 2, o_dk, slab_peers, True)
        arrive(gnear.at[i, 1, cross_rows, :], rd.at[i, 1])
        settle(i, 1, cross_rows)
        gather(i, 3, o_dv, slab_peers[:2], False)
        arrive(gnear.at[i, 1, local_rows, :], rd.at[i, 2])
        settle(i, 1, local_rows)
        gather(i, 3, o_dv, slab_peers[2:], True)

    def ship_on(i):
        ship_cross(i)

        @pl.when(i + 1 < heads)
        def _():
            ship_held(i + 1)
            ship_beside(i + 1)

    listing_copy = pltpu.make_async_copy(listing, nbr, nbr_in)
    listing_copy.start()

    spread_kv(0)
    ship_held(0)
    spread_kv(1)
    ship_held(1)
    spread_kv(2)
    for i in range(3, heads):
        spread_qd(i - 3)
        spread_kv(i)
    for i in range(max(heads - 3, 0), heads):
        spread_qd(i)

    @pl.when(first == 0)
    def _():
        signal(ready.at[odd], (below, h))

    @pl.when((last == 1) & (s < n - 2))
    def _():
        signal(ready.at[1 - odd], (above, h))

    ship_beside(0)
    ship_beside(1)

    listing_copy.wait()
    lane_tile = lax.broadcasted_iota(jnp.int32, (8, rows), 1) // TILE
    far_first = jnp.where(s == 0, -1000, (s - 1 + 2 * odd) * tiles)
    firsts = (s * tiles, near * tiles, far_first)
    listed = []
    for slot in range(nbr.shape[1]):
        row = jnp.full((8, rows), nbr[0, slot], jnp.int32)
        for t in range(1, tiles):
            row = jnp.where(lane_tile == t, nbr[t, slot], row)
        listed.append(row)
    for b in range(3):
        for t in range(tiles):
            hit = listed[0] == firsts[b] + t
            for row in listed[1:]:
                hit = hit | (row == firsts[b] + t)
            bias[b * tiles + t] = jnp.where(hit, 0.0, NEG)

    ship_cross(0)
    ship_on(1)

    @pl.when((jnp.where(odd == 0, 1 - last, first) == 1) & (s != 1))
    def _():
        pl.semaphore_wait(ready.at[0], 1)

    relay(0)
    ship_on(2)

    hold = jnp.where((s > 0) & (odd == 0), 2 * first, 0)

    @pl.loop(0, heads + 6)
    def _(step):
        for start, lag, task, here in ((1, -1, relay, True), (3, -3, ship_on, last == 0), (0, 3, fold, True),
                                       (0, hold, compute, True), (3, -3, ship_on, last == 1), (0, 6, finish, True)):
            i = step - lag

            @pl.when((i >= start) & (i < heads) & here)
            def _():
                task(i)

    for i in range(heads):
        arrive(kv.at[0, i, :, 0 : 3 * block], kv_out.at[i])
        arrive(qd.at[i, :, 0 : 3 * block], qd_out.at[i])
        arrive(kv.at[0, i], sa.at[i])
        arrive(near16.at[i], sd.at[i])
    @pl.when(jnp.logical_not(single))
    def _():
        for i in range(heads):
            arrive(kv.at[1, i], sb.at[i])

    @pl.when(jnp.logical_not(lone))
    def _():
        for i in range(heads):
            arrive(far16.at[i], sc.at[i])

    for a in range(4):
        arrive(outs.at[a, :, 0 : 3 * block], so.at[a])
        arrive(outs.at[a, :, 0 : 3 * block], ro.at[a])
        arrive(outs.at[a, :, 0:block], lo.at[a])


def solution(mesh):
    n = mesh.shape["slab"]
    parts = mesh.shape["head"]

    def step(query_in, key_in, value_in, grad_out, neighbours):
        block, full = query_in.shape
        rows = block * parts
        heads = full // parts // HD
        tiles = rows // TILE
        shape = jax.ShapeDtypeStruct((block, full), BF16)
        pair16 = pltpu.VMEM((heads, 2, rows, HD), BF16)
        pair32 = pltpu.VMEM((heads, 2, rows, HD), F32)
        each = pltpu.SemaphoreType.DMA((heads,))
        four = pltpu.SemaphoreType.DMA((4,))
        held = pl.pallas_call(
            functools.partial(kernel, n),
            out_shape=(pltpu.VMEM((block, full), BF16),) * 4,
            in_specs=[pl.BlockSpec(memory_space=pl.ANY)] * 5,
            out_specs=(pl.BlockSpec(memory_space=pltpu.VMEM),) * 4,
            scratch_shapes=[
                pltpu.VMEM((3, heads, 2, rows, HD), BF16),
                pair16,
                pltpu.VMEM((3 * tiles, 8, rows), F32),
                pltpu.VMEM((3 * rows, rows), F32),
                pltpu.VMEM((3 * rows, rows), BF16),
                pair32, pair32,
                pair16, pair16, pair16, pair16,
                pltpu.VMEM((4, heads, rows, HD), BF16),
            ] + [each] * 11 + [pltpu.SemaphoreType.DMA((heads, 2)), each]
            + [pltpu.SemaphoreType.DMA((heads, 3))] + [four] * 3
            + [pltpu.SemaphoreType.REGULAR((2,)), pltpu.SMEM(neighbours.shape, jnp.int32),
               pltpu.SemaphoreType.DMA],
            compiler_params=pltpu.CompilerParams(
                collective_id=0, has_side_effects=True, vmem_limit_bytes=61 * 1024 * 1024 + 512 * 1024
            ),
        )(neighbours, query_in, key_in, value_in, grad_out)
        return held

    rows_spec = P(("slab", "head"), None)
    return jax.shard_map(
        step, mesh=mesh, in_specs=(rows_spec,) * 4 + (P("slab", None),),
        out_specs=(rows_spec,) * 4, check_vma=False,
    )
```

```python
import functools
import math

import jax
import jax.numpy as jnp
from jax import lax
from jax.experimental import pallas as pl
from jax.experimental.pallas import tpu as pltpu
from jax.sharding import PartitionSpec as P

HD = 128
TILE = 64
MESH = pl.DeviceIdType.MESH
F32 = jnp.float32
BF16 = jnp.bfloat16
NEG = -1e30

NN = (((1,), (0,)), ((), ()))
NT = (((1,), (1,)), ((), ()))
TN = (((0,), (0,)), ((), ()))


def dot(a, b, dims):
    return lax.dot_general(a, b, dims, preferred_element_type=F32)


def attend_head(i, kv, qd, bias, s_scr, p_scr, own32, near32, far16, outs):
    rows = qd.shape[2]
    tiles = rows // TILE
    scale = 1.0 / math.sqrt(HD)
    c = scale * math.log2(math.e)
    query = qd[i, 0]
    peak = None
    for b in range(3):
        s = dot(kv[b, i, 0], query, NT)
        s = s.reshape(tiles, TILE // 8, 8, rows) + bias[b * tiles : (b + 1) * tiles][:, None]
        top = jnp.max(s, axis=(0, 1))
        peak = top if peak is None else jnp.maximum(peak, top)
        s_scr[b * rows : (b + 1) * rows] = s.reshape(rows, rows)
    peak = jnp.max(peak, axis=0, keepdims=True)
    total = None
    out_t = None
    for b in range(3):
        part = slice(b * rows, (b + 1) * rows)
        e = jnp.exp2((s_scr[part] - peak) * c)
        t = jnp.sum(e.reshape(rows // 8, 8, rows), axis=0)
        total = t if total is None else total + t
        low = e.astype(BF16)
        p_scr[part] = low
        s_scr[part] = e
        o = dot(kv[b, i, 1], low, TN)
        out_t = o if out_t is None else out_t + o
    inv = 1.0 / jnp.sum(total, axis=0, keepdims=True)
    out_low = (out_t * inv).astype(BF16).astype(F32)
    outs[0, i] = out_low.T.astype(BF16)
    grad_t = qd[i, 1].astype(F32).T * inv
    grad_n = grad_t.T.astype(BF16)
    delta = jnp.sum(grad_t * out_low, axis=0, keepdims=True)
    dq_t = None
    for b in range(3):
        part = slice(b * rows, (b + 1) * rows)
        dp = dot(kv[b, i, 1], grad_n, NT)
        ds = (s_scr[part] * (dp - delta)).astype(BF16)
        dk = dot(ds, query, NN) * scale
        dv = dot(p_scr[part], grad_n, NN)
        if b == 2:
            far16[i, 0] = dk.astype(BF16)
            far16[i, 1] = dv.astype(BF16)
        else:
            held = own32 if b == 0 else near32
            held[i, 0] = dk
            held[i, 1] = dv
        g = dot(kv[b, i, 0], ds, TN)
        dq_t = g if dq_t is None else dq_t + g
    outs[1, i] = (dq_t * scale).T.astype(BF16)


def kernel(n, listing, q, k, v, do, o_att, o_dq, o_dk, o_dv,
           kv, qd, bias, s_scr, p_scr, own32, near32, far16, near16, gfar, gnear, outs,
           kv_own, kv_beside, kv_cross, kv_out, qd_in, qd_out,
           sa, ra, sb, rb, sc, rc, sd, rd, so, ro, lo, ready, nbr, nbr_in):
    block = q.shape[0]
    rows = qd.shape[2]
    heads = qd.shape[0]
    tiles = rows // TILE
    width = heads * HD
    s = lax.axis_index("slab")
    h = lax.axis_index("head")
    odd = lax.rem(s, 2)
    near = s + 1 - 2 * odd
    above = lax.rem(s + 2, n)
    below = lax.rem(s - 2 + n, n)
    onward = jnp.where(odd == 0, above, below)
    source = jnp.where(odd == 0, below, above)
    across = lax.rem(h + 2, 4)
    beside = h + 1 - 2 * lax.rem(h, 2)
    slab_peers = (s, across), (s, lax.rem(beside + 2, 4)), (s, beside)
    near_id, onward_id, source_id = (near, across), (onward, h), (source, h)
    depth = min(16, n // 2)
    level = lax.rem(s // 2, depth)
    first = jnp.where(level == 0, 1, 0)
    last = jnp.where(level == depth - 1, 1, 0)
    lone = (s == 0) | (s == n - 1)
    single = (s == 1) | (s == n - 2)

    def group(head):
        return lax.rem(head + 2 * odd, 4)

    def columns(head, i):
        return pl.ds(pl.multiple_of(group(head) * width + i * HD, HD), HD)

    def block_of(head):
        return pl.ds(pl.multiple_of(head * block, 32), block)

    cross_rows = pl.ds(pl.multiple_of((1 - h // 2) * (2 * block), 32), 2 * block)
    local_rows = pl.ds(pl.multiple_of((h // 2) * (2 * block), 32), 2 * block)

    def signal(sem, peer):
        pl.semaphore_signal(sem, inc=1, device_id=peer, device_id_type=MESH)

    barrier = pltpu.get_barrier_semaphore()
    for peer in slab_peers + (near_id,):
        signal(barrier, peer)

    @pl.when(last == 0)
    def _():
        signal(barrier, (above, h))

    @pl.when(first == 1)
    def _():
        signal(barrier, (below, h))

    pl.semaphore_wait(barrier, 5 - first + last)

    def send(src, dst, s_sem, r_sem, peer):
        pltpu.make_async_remote_copy(
            src_ref=src, dst_ref=dst, send_sem=s_sem, recv_sem=r_sem,
            device_id=peer, device_id_type=MESH,
        ).start()

    def arrive(ref, sem):
        pltpu.make_async_copy(ref, ref, sem).wait()

    def spread(i, pair, into, out, sems, mine):
        for peer, sem in zip(slab_peers, sems):
            for a, ref in enumerate(pair):
                send(ref.at[:, columns(peer[1], i)], into.at[i, a, block_of(h), :],
                     out.at[i], sem.at[i], peer)
        for a, ref in enumerate(pair):
            pltpu.make_async_copy(
                ref.at[:, columns(h, i)], into.at[i, a, block_of(h), :], mine.at[i]
            ).start()

    def spread_kv(i):
        spread(i, (k, v), kv.at[0], kv_out, (kv_cross, kv_cross, kv_beside), kv_own)

    def spread_qd(i):
        spread(i, (q, do), qd, qd_out, (qd_in, qd_in, qd_in), qd_in)

    def ship_held(i):
        for a, ref in enumerate((k, v)):
            send(ref.at[:, columns(h, i)], kv.at[1, i, a, block_of(h), :], sa.at[i], ra.at[i], near_id)

    def ship_beside(i):
        part = kv.at[0, i, :, block_of(beside), :]
        arrive(part, kv_beside.at[i])
        send(part, kv.at[1, i, :, block_of(beside), :], sa.at[i], ra.at[i], near_id)

    def ship_cross(i):
        part = kv.at[0, i, :, cross_rows, :]
        arrive(part, kv_cross.at[i])
        send(part, kv.at[1, i, :, cross_rows, :], sa.at[i], ra.at[i], near_id)

    def gather(i, a, out, peers, mine):
        for peer in peers:
            send(outs.at[a, i, block_of(peer[1]), :], out.at[:, columns(h, i)],
                 so.at[a], ro.at[a], peer)
        if mine:
            pltpu.make_async_copy(
                outs.at[a, i, block_of(h), :], out.at[:, columns(h, i)], lo.at[a]
            ).start()

    def relay(i):
        arrive(kv.at[1, i], ra.at[i])

        @pl.when(jnp.logical_not(single))
        def _():
            send(kv.at[1, i], kv.at[2, i], sb.at[i], rb.at[i], onward_id)

        @pl.when(lone)
        def _():
            pltpu.make_async_copy(kv.at[1, i], kv.at[2, i], rb.at[i]).start()

    def compute(i):
        arrive(kv.at[0, i, :, block_of(h), :], kv_own.at[i])
        arrive(qd.at[i], qd_in.at[i])
        arrive(kv.at[2, i], rb.at[i])
        attend_head(i, kv, qd, bias, s_scr, p_scr, own32, near32, far16, outs)

        @pl.when((i == 0) & (jnp.where(odd == 0, first, 1 - last) == 1) & (s > 0))
        def _():
            pl.semaphore_wait(ready.at[1], 1)

        @pl.when(jnp.logical_not(lone))
        def _():
            for a in range(2):
                send(far16.at[i, a], gfar.at[i, a], sc.at[i], rc.at[i, a], source_id)

        gather(i, 0, o_att, slab_peers, True)
        gather(i, 1, o_dq, slab_peers, True)

    def fold(i):
        for a in range(2):
            @pl.when(jnp.logical_not(single))
            def _():
                arrive(gfar.at[i, a], rc.at[i, a])
                near16[i, a] = (near32[i, a] + gfar[i, a].astype(F32)).astype(BF16)

            @pl.when(single)
            def _():
                near16[i, a] = near32[i, a].astype(BF16)

            if a == 0:
                send(near16.at[i, a], gnear.at[i, a], sd.at[i], rd.at[i, a], near_id)
            else:
                for piece, part in ((1, local_rows), (2, cross_rows)):
                    send(near16.at[i, a, part, :], gnear.at[i, a, part, :], sd.at[i], rd.at[i, piece], near_id)

    def settle(i, a, part):
        outs[2 + a, i, part, :] = (own32[i, a, part, :] + gnear[i, a, part, :].astype(F32)).astype(BF16)

    def finish(i):
        arrive(gnear.at[i, 0], rd.at[i, 0])
        settle(i, 0, slice(None))
        gather(i, 2, o_dk, slab_peers, True)
        arrive(gnear.at[i, 1, cross_rows, :], rd.at[i, 1])
        settle(i, 1, cross_rows)
        gather(i, 3, o_dv, slab_peers[:2], False)
        arrive(gnear.at[i, 1, local_rows, :], rd.at[i, 2])
        settle(i, 1, local_rows)
        gather(i, 3, o_dv, slab_peers[2:], True)

    def ship_on(i):
        ship_cross(i)

        @pl.when(i + 1 < heads)
        def _():
            ship_held(i + 1)
            ship_beside(i + 1)

    listing_copy = pltpu.make_async_copy(listing, nbr, nbr_in)
    listing_copy.start()

    spread_kv(0)
    ship_held(0)
    spread_kv(1)
    ship_held(1)
    spread_kv(2)
    for i in range(3, heads):
        spread_qd(i - 3)
        spread_kv(i)
    for i in range(max(heads - 3, 0), heads):
        spread_qd(i)

    @pl.when(first == 0)
    def _():
        signal(ready.at[odd], (below, h))

    @pl.when((last == 1) & (s < n - 2))
    def _():
        signal(ready.at[1 - odd], (above, h))

    ship_beside(0)
    ship_beside(1)

    listing_copy.wait()
    lane_tile = lax.broadcasted_iota(jnp.int32, (8, rows), 1) // TILE
    far_first = jnp.where(s == 0, -1000, (s - 1 + 2 * odd) * tiles)
    firsts = (s * tiles, near * tiles, far_first)
    listed = []
    for slot in range(nbr.shape[1]):
        row = jnp.full((8, rows), nbr[0, slot], jnp.int32)
        for t in range(1, tiles):
            row = jnp.where(lane_tile == t, nbr[t, slot], row)
        listed.append(row)
    for b in range(3):
        for t in range(tiles):
            hit = listed[0] == firsts[b] + t
            for row in listed[1:]:
                hit = hit | (row == firsts[b] + t)
            bias[b * tiles + t] = jnp.where(hit, 0.0, NEG)

    ship_cross(0)
    ship_on(1)

    @pl.when((jnp.where(odd == 0, 1 - last, first) == 1) & (s != 1))
    def _():
        pl.semaphore_wait(ready.at[0], 1)

    relay(0)
    ship_on(2)

    hold = jnp.where((s > 0) & (odd == 0), 2 * first, 0)

    @pl.loop(0, heads + 4)
    def _(step):
        for start, lag, task, here in ((1, -1, relay, True), (3, -3, ship_on, last == 0), (0, 3, fold, True),
                                       (0, hold, compute, True), (3, -3, ship_on, last == 1), (0, 4, finish, True)):
            i = step - lag

            @pl.when((i >= start) & (i < heads) & here)
            def _():
                task(i)

    for i in range(heads):
        arrive(kv.at[0, i, :, 0 : 3 * block], kv_out.at[i])
        arrive(qd.at[i, :, 0 : 3 * block], qd_out.at[i])
        arrive(kv.at[0, i], sa.at[i])
        arrive(near16.at[i], sd.at[i])
    @pl.when(jnp.logical_not(single))
    def _():
        for i in range(heads):
            arrive(kv.at[1, i], sb.at[i])

    @pl.when(jnp.logical_not(lone))
    def _():
        for i in range(heads):
            arrive(far16.at[i], sc.at[i])

    for a in range(4):
        arrive(outs.at[a, :, 0 : 3 * block], so.at[a])
        arrive(outs.at[a, :, 0 : 3 * block], ro.at[a])
        arrive(outs.at[a, :, 0:block], lo.at[a])


def solution(mesh):
    n = mesh.shape["slab"]
    parts = mesh.shape["head"]

    def step(query_in, key_in, value_in, grad_out, neighbours):
        block, full = query_in.shape
        rows = block * parts
        heads = full // parts // HD
        tiles = rows // TILE
        shape = jax.ShapeDtypeStruct((block, full), BF16)
        pair16 = pltpu.VMEM((heads, 2, rows, HD), BF16)
        pair32 = pltpu.VMEM((heads, 2, rows, HD), F32)
        each = pltpu.SemaphoreType.DMA((heads,))
        four = pltpu.SemaphoreType.DMA((4,))
        held = pl.pallas_call(
            functools.partial(kernel, n),
            out_shape=(pltpu.VMEM((block, full), BF16),) * 4,
            in_specs=[pl.BlockSpec(memory_space=pl.ANY)] * 5,
            out_specs=(pl.BlockSpec(memory_space=pltpu.VMEM),) * 4,
            scratch_shapes=[
                pltpu.VMEM((3, heads, 2, rows, HD), BF16),
                pair16,
                pltpu.VMEM((3 * tiles, 8, rows), F32),
                pltpu.VMEM((3 * rows, rows), F32),
                pltpu.VMEM((3 * rows, rows), BF16),
                pair32, pair32,
                pair16, pair16, pair16, pair16,
                pltpu.VMEM((4, heads, rows, HD), BF16),
            ] + [each] * 11 + [pltpu.SemaphoreType.DMA((heads, 2)), each]
            + [pltpu.SemaphoreType.DMA((heads, 3))] + [four] * 3
            + [pltpu.SemaphoreType.REGULAR((2,)), pltpu.SMEM(neighbours.shape, jnp.int32),
               pltpu.SemaphoreType.DMA],
            compiler_params=pltpu.CompilerParams(
                collective_id=0, has_side_effects=True, vmem_limit_bytes=61 * 1024 * 1024 + 512 * 1024
            ),
        )(neighbours, query_in, key_in, value_in, grad_out)
        return held

    rows_spec = P(("slab", "head"), None)
    return jax.shard_map(
        step, mesh=mesh, in_specs=(rows_spec,) * 4 + (P("slab", None),),
        out_specs=(rows_spec,) * 4, check_vma=False,
    )
```
